128 devices in a mesh: seq: 32 (over y, z, core), wide: 4 (over x).
Axes of the slice: x: 4, y: 4, z: 4, core: 2. Of those that a mesh axis runs over, the one named last changes fastest.
Arguments:
- tokens: bfloat16 [49152, 1024], P('seq'), may hold values from -81 to 81
- shared_weight: bfloat16 [1024, 1024], P(None, 'wide'), may hold values from -0.1875 to 0.1875
- value_weight: bfloat16 [1024, 1024], P(None, 'wide'), may hold values from -0.1875 to 0.1875
- output_weight: bfloat16 [1024, 1024], P('wide'), may hold values from -0.1875 to 0.1875
- cotangent: bfloat16 [49152, 1024], P('seq'), may hold values from -6 to 6
- block_clusters: int32 [4, 384], P('wide', 'seq'), may hold values from 0 to 255, as said below
Outputs:
- token_grads: bfloat16 [49152, 1024], P('seq', 'wide')
- shared_grads: float32 [1024, 1024], P('seq', 'wide')
- value_grads: float32 [1024, 1024], P('seq', 'wide')
- output_grads: float32 [1024, 1024], P('wide', 'seq')
The draws below stay inside these ranges and needn't reach their ends.
Inputs may be any that keep to these rules, and one draw needn't show every extreme that they name: `block_clusters`: group o holds clusters o * 8 to (o + 1) * 8 - 1. For each routed head: the blocks of one device along seq have at most 2 blocks in the clusters of any one group; some group receives exactly 2 blocks from every device, and each of its clusters then holds 8 blocks; no cluster holds more than 8 blocks.
All inputs are finite; a program needn't handle non-finite values.
Results may differ from the reference program's by a relative error of at most 0.012.
The reference program's roundings to bfloat16 on the way count: a program that leaves them out, or rounds other values in their place, can miss the bound.
Values may be sent and summed in bfloat16 or wider, within the bound.
A program may use at most 128 MiB of HBM per device.

```python
import math
import jax
import jax.numpy as jnp
from jax import lax

D = 1024
HEAD = 128
HEAD_PAIRS = 4
WINDOW = 256
BLOCK = 128
CLUS_DEV = 8
TOK_DEV = 1536
SCAP = 2
TOKENS = 49152
NBLOCKS = 384
CLUSTERS = 256
CAPC = 8


def draw_tokens(key, part):
    return jnp.clip(jax.random.normal(key, (TOKENS, D), jnp.float32), -5.0, 5.0).astype(jnp.bfloat16)


def draw_block_clusters(key, part):
    seq_devices = TOKENS // TOK_DEV
    block_local = TOK_DEV // BLOCK
    slot_total = seq_devices * SCAP
    capacity = slot_total // CLUS_DEV
    block_order = jnp.arange(block_local)

    def one_source(source_key, hot_owner):
        first_key, second_key = jax.random.split(source_key)
        virtual = jax.random.permutation(first_key, (seq_devices - 1) * SCAP)[:block_local - SCAP]
        others = (hot_owner + 1 + virtual // SCAP) % seq_devices
        owners = jnp.concatenate([jnp.full((SCAP,), hot_owner, dtype=jnp.int32), others.astype(jnp.int32)])
        return owners[jax.random.permutation(second_key, block_local)]

    def one_head(head_key):
        hot_key, source_key, owner_key = jax.random.split(head_key, 3)
        hot_owner = jax.random.randint(hot_key, (), 0, seq_devices)
        owners = jax.vmap(lambda each_key: one_source(each_key, hot_owner))(jax.random.split(source_key, seq_devices))
        same_owner = owners[:, :, None] == owners[:, None, :]
        earlier = block_order[None, :] < block_order[:, None]
        block_ranks = jnp.sum(same_owner & earlier[None, :, :], axis=2)
        virtual_slot = jnp.arange(seq_devices)[:, None] * SCAP + block_ranks
        slot_perms = jax.vmap(lambda each_key: jax.random.permutation(each_key, slot_total))(jax.random.split(owner_key, seq_devices))
        picked = slot_perms[owners, virtual_slot] // capacity
        return (owners * CLUS_DEV + picked).reshape(-1).astype(jnp.int32)
    return jax.vmap(one_head)(jax.random.split(key, HEAD_PAIRS))


def with_spikes(values, stream_key, source, target, blocks, factor):
    def block_of(position):
        return (jnp.arange(values.shape[position]) // (values.shape[position] // blocks)).reshape((-1,) + (1,) * (values.ndim - 1 - position))

    near = jax.random.permutation(stream_key, blocks)[block_of(target)]
    far = (block_of(target) + blocks // 2) % blocks
    return jnp.where((block_of(source) == near) | (block_of(source) == far), factor * values, values)


def levels(rng, extent, cuts, low, high):
    def one(axis_at, shards_of):
        heights = jax.random.uniform(jax.random.fold_in(jax.random.fold_in(rng, 6), axis_at), (shards_of,), jnp.float32, low / len(cuts), high / len(cuts))
        return jnp.repeat(jnp.exp(heights), extent[axis_at] // shards_of).reshape((-1,) + (1,) * (len(extent) - axis_at - 1))

    gain = one(*cuts[0])
    for cut in cuts[1:]:
        gain = gain * one(*cut)
    return gain


def normal_values(rng, shape, deviation, limit, shards=(), kind=jnp.bfloat16):
    drawn = deviation * jax.random.normal(rng, shape, jnp.float32)
    if shards:
        drawn = drawn * levels(rng, shape, shards, -0.22, 0.18)
    return jnp.clip(drawn, -limit, limit).astype(kind)


def noise_with(rng, shape, deviation, bound, shards, heavy, kind=jnp.bfloat16):
    drawn = deviation * jax.random.normal(rng, shape, jnp.float32)
    if shards:
        drawn = drawn * levels(rng, shape, shards, -0.22, 0.18)
    return jnp.clip(with_spikes(drawn, jax.random.fold_in(rng, 3), *heavy), -bound, bound).astype(kind)


def setup_inputs(seed: int = 0) -> dict:
    arg_keys = jax.random.split(jax.random.key(seed), 7)
    return {
        "tokens": draw_tokens(jax.random.fold_in(arg_keys[6], 71), 0),
        "shared_weight": normal_values(arg_keys[1], (D, D), D ** -0.5, 0.1875, ((1, 4),)),
        "value_weight": normal_values(arg_keys[2], (D, D), D ** -0.5, 0.1875, ((1, 4),)),
        "output_weight": normal_values(arg_keys[3], (D, D), D ** -0.5, 0.1875, ((0, 4),)),
        "cotangent": noise_with(arg_keys[4], (TOKENS, D), 1.0, 6.0, ((0, 32),), (0, 1, 32, 2.75)),
        "block_clusters": draw_block_clusters(jax.random.fold_in(arg_keys[6], 71), 0),
    }


EPSILON = 1e-06
NEGATIVE = -1e+30

def contract(left_side, right_side, left_dim, right_dim):
    return lax.dot_general(left_side, right_side, (((left_dim,), (right_dim,)), ((), ())), preferred_element_type=jnp.float32)

def unit_keys(queries):
    floats = queries.astype(jnp.float32)
    factor = lax.rsqrt(lax.optimization_barrier(jnp.mean(floats * floats, axis=-1, keepdims=True)) + EPSILON)
    return ((floats * factor).astype(jnp.bfloat16), factor)

def key_chain(queries, factor, key_grads):
    floats = queries.astype(jnp.float32)
    inner_sum = lax.optimization_barrier(jnp.sum(floats * key_grads, axis=-1, keepdims=True))
    return factor * key_grads - factor ** 3 / floats.shape[-1] * floats * inner_sum

def attend(queries, key_rows, values, cotangent_rows, allowed, self_spot, want_grads):
    head_scale = 1.0 / math.sqrt(queries.shape[-1])
    scores = contract(queries, key_rows, 1, 1) * head_scale
    scores = jnp.where(self_spot, 0.0, scores)
    scores = jnp.where(allowed, scores, NEGATIVE)
    highest = lax.optimization_barrier(jnp.max(scores, axis=1, keepdims=True))
    weights = jnp.where(allowed, jnp.exp(scores - highest), 0.0)
    probs_full = weights / lax.optimization_barrier(jnp.sum(weights, axis=1, keepdims=True))
    probs_half = probs_full.astype(jnp.bfloat16)
    outputs = contract(probs_half, values, 1, 0).astype(jnp.bfloat16)
    if not want_grads:
        return outputs
    prob_grads = contract(cotangent_rows, values, 1, 1)
    centre = lax.optimization_barrier(jnp.sum(probs_full * prob_grads, axis=1, keepdims=True))
    score_grads = jnp.where(self_spot, 0.0, probs_full * (prob_grads - centre))
    score_half = (score_grads * head_scale).astype(jnp.bfloat16)
    query_grads = contract(score_half, key_rows, 1, 0)
    key_grads = contract(score_half, queries, 0, 0)
    value_grads = contract(probs_half, cotangent_rows, 0, 0)
    return (outputs, query_grads, key_grads, value_grads)

def band_pass(query_ext, value_ext, tangent_ext, first_position, seq_tokens, window, tile_rows):
    length = query_ext.shape[0]
    feature_width = query_ext.shape[1]
    queries_count = length - window
    tile_total = -(-queries_count // tile_rows)
    padded = window + tile_total * tile_rows
    pad_rows = padded - length
    query_pad = jnp.pad(query_ext, ((0, pad_rows), (0, 0)))
    value_pad = jnp.pad(value_ext, ((0, pad_rows), (0, 0)))
    tangent_pad = jnp.pad(tangent_ext, ((0, pad_rows), (0, 0)))
    key_pad, factor = unit_keys(query_pad)
    rows_at = jnp.arange(padded, dtype=jnp.int32)
    positions = first_position + rows_at
    usable = (positions >= 0) & (positions < seq_tokens) & (rows_at < length)
    offsets = window + jnp.arange(tile_rows, dtype=jnp.int32)[:, None] - jnp.arange(tile_rows + window, dtype=jnp.int32)[None, :]
    in_band = (offsets >= 0) & (offsets <= window)
    self_spot = offsets == 0

    def visit_tile(tile_index, carried):
        key_sums, value_sums, out_rows, query_rows = carried
        tile_start = (tile_index * tile_rows).astype(jnp.int32)
        queries = lax.dynamic_slice_in_dim(query_pad, tile_start + window, tile_rows, 0)
        key_rows = lax.dynamic_slice_in_dim(key_pad, tile_start, tile_rows + window, 0)
        values = lax.dynamic_slice_in_dim(value_pad, tile_start, tile_rows + window, 0)
        tangents = lax.dynamic_slice_in_dim(tangent_pad, tile_start + window, tile_rows, 0)
        key_usable = lax.dynamic_slice_in_dim(usable, tile_start, tile_rows + window, 0)
        allowed = in_band & key_usable[None, :] | self_spot
        outputs, query_grads, key_grads, value_grads = attend(queries, key_rows, values, tangents, allowed, self_spot, True)
        old_keys = lax.dynamic_slice_in_dim(key_sums, tile_start, tile_rows + window, 0)
        key_sums = lax.dynamic_update_slice_in_dim(key_sums, old_keys + key_grads, tile_start, 0)
        old_values = lax.dynamic_slice_in_dim(value_sums, tile_start, tile_rows + window, 0)
        value_sums = lax.dynamic_update_slice_in_dim(value_sums, old_values + value_grads, tile_start, 0)
        out_rows = lax.dynamic_update_slice_in_dim(out_rows, outputs, tile_start, 0)
        query_rows = lax.dynamic_update_slice_in_dim(query_rows, query_grads, tile_start, 0)
        return (key_sums, value_sums, out_rows, query_rows)
    initial = (jnp.zeros((padded, feature_width), jnp.float32), jnp.zeros((padded, feature_width), jnp.float32), jnp.zeros((tile_total * tile_rows, feature_width), jnp.bfloat16), jnp.zeros((tile_total * tile_rows, feature_width), jnp.float32))
    key_sums, value_sums, out_rows, query_rows = lax.fori_loop(0, tile_total, visit_tile, initial)
    return (out_rows[:queries_count], query_rows[:queries_count], key_sums[:length], value_sums[:length], factor[:length])

def cluster_pass(packed, want_grads):
    row_count = packed.shape[0]
    queries = packed[:, :HEAD]
    values = packed[:, HEAD:2 * HEAD]
    key_rows, factor = unit_keys(queries)
    row_order = jnp.arange(row_count, dtype=jnp.int32)
    allowed = row_order[None, :] <= row_order[:, None]
    self_spot = row_order[None, :] == row_order[:, None]
    if not want_grads:
        return attend(queries, key_rows, values, None, allowed, self_spot, False)
    tangents = packed[:, 2 * HEAD:]
    outputs, query_grads, key_grads, value_grads = attend(queries, key_rows, values, tangents, allowed, self_spot, True)
    query_total = (query_grads + key_chain(queries, factor, key_grads)).astype(jnp.bfloat16)
    return jnp.concatenate([outputs, query_total, value_grads.astype(jnp.bfloat16)], axis=1)

def full_pass(cluster_rows):
    return cluster_pass(cluster_rows, True)

def local_head(queries, values, tangents):
    zero_rows = jnp.zeros((WINDOW, HEAD), jnp.bfloat16)
    query_ext = jnp.concatenate([zero_rows, queries], axis=0)
    value_ext = jnp.concatenate([zero_rows, values], axis=0)
    tangent_ext = jnp.concatenate([zero_rows, tangents], axis=0)
    outputs, query_grads, key_grads, value_grads, factor = band_pass(query_ext, value_ext, tangent_ext, -WINDOW, TOKENS, WINDOW, min(512, TOK_DEV))
    query_total = (query_grads + key_chain(queries, factor[WINDOW:], key_grads[WINDOW:])).astype(jnp.bfloat16)
    return (outputs, query_total, value_grads[WINDOW:].astype(jnp.bfloat16))

def routed_head(queries, values, tangents, labels):
    block_order = jnp.arange(NBLOCKS, dtype=jnp.int32)
    block_ranks = lax.optimization_barrier(jnp.sum((labels[None, :] == labels[:, None]) & (block_order[None, :] < block_order[:, None]), axis=1)).astype(jnp.int32)
    slots = (labels * CAPC + block_ranks).astype(jnp.int32)
    grid_slots = jnp.arange(CLUSTERS * CAPC, dtype=jnp.int32)
    slot_hits = slots[None, :] == grid_slots[:, None]
    sources = lax.optimization_barrier(jnp.sum(jnp.where(slot_hits, block_order[None, :], 0), axis=1)).astype(jnp.int32)
    present = jnp.any(slot_hits, axis=1)
    packed = jnp.concatenate([queries, values, tangents], axis=1).reshape(NBLOCKS, BLOCK, 3 * HEAD)
    buffer = jnp.where(present[:, None, None], packed[sources], 0).reshape(CLUSTERS, CAPC * BLOCK, 3 * HEAD)
    results = lax.map(full_pass, buffer)
    results = results.reshape(CLUSTERS * CAPC, BLOCK, 3 * HEAD)[slots].reshape(TOKENS, 3 * HEAD)
    return (results[:, :HEAD], results[:, HEAD:2 * HEAD], results[:, 2 * HEAD:])

def reference(tokens, shared_weight, value_weight, output_weight, cotangent, block_clusters):
    shared = contract(tokens, shared_weight, 1, 0).astype(jnp.bfloat16)
    valued = contract(tokens, value_weight, 1, 0).astype(jnp.bfloat16)
    head_cotangent = contract(cotangent, output_weight, 1, 1).astype(jnp.bfloat16)
    out_list, query_list, value_list = ([], [], [])
    for pair_index in range(HEAD_PAIRS):
        local_cols = slice(2 * pair_index * HEAD, (2 * pair_index + 1) * HEAD)
        routed_cols = slice((2 * pair_index + 1) * HEAD, (2 * pair_index + 2) * HEAD)
        local_out, local_dq, local_dv = local_head(shared[:, local_cols], valued[:, local_cols], head_cotangent[:, local_cols])
        routed_out, routed_dq, routed_dv = routed_head(shared[:, routed_cols], valued[:, routed_cols], head_cotangent[:, routed_cols], block_clusters[pair_index])
        out_list += [local_out, routed_out]
        query_list += [local_dq, routed_dq]
        value_list += [local_dv, routed_dv]
    attended = jnp.concatenate(out_list, axis=1)
    query_all = jnp.concatenate(query_list, axis=1)
    value_all = jnp.concatenate(value_list, axis=1)
    token_grads = (contract(query_all, shared_weight, 1, 1) + contract(value_all, value_weight, 1, 1)).astype(jnp.bfloat16)
    grad_scale = 1.0 / math.sqrt(TOKENS)
    shared_grads = contract(tokens, query_all, 0, 0) * grad_scale
    value_grads = contract(tokens, value_all, 0, 0) * grad_scale
    output_grads = contract(attended, cotangent, 0, 0) * grad_scale
    return (token_grads, shared_grads, value_grads, output_grads)
```

```python
import functools
import math

import jax
import jax.numpy as jnp
from jax import lax
from jax.experimental import pallas as pl
from jax.experimental.pallas import tpu as pltpu
from jax.sharding import PartitionSpec as P

HEAD = 128
WINDOW = 256
BLOCK = 128
MOST = 8
SLOTS = 16

EPSILON = 1e-06
NEGATIVE = -1e30
TILE = 256


def contract(left_side, right_side, left_dim, right_dim):
    return lax.dot_general(
        left_side,
        right_side,
        (((left_dim,), (right_dim,)), ((), ())),
        preferred_element_type=jnp.float32,
    )


def unit_factor(floats):
    return lax.rsqrt(jnp.mean(floats * floats, axis=-1, keepdims=True) + EPSILON)


def chain(floats, key_grads):
    factor = unit_factor(floats)
    inner_sum = jnp.sum(floats * key_grads, axis=-1, keepdims=True)
    return factor * key_grads - factor**3 / HEAD * floats * inner_sum


def attend(queries, keys, values, tangents, allowed, self_spot):
    head_scale = 1.0 / math.sqrt(HEAD)
    scores = contract(queries, keys, 1, 1) * head_scale
    scores = jnp.where(self_spot, 0.0, scores)
    scores = jnp.where(allowed, scores, NEGATIVE)
    highest = jnp.max(scores, axis=1, keepdims=True)
    weights = jnp.exp(scores - highest)
    probs = weights * (1.0 / jnp.sum(weights, axis=1, keepdims=True))
    probs_half = probs.astype(jnp.bfloat16)
    outputs = contract(probs_half, values, 1, 0)
    prob_grads = contract(tangents, values, 1, 1)
    centre = jnp.sum(probs * prob_grads, axis=1, keepdims=True)
    score_grads = jnp.where(self_spot, 0.0, probs * (prob_grads - centre))
    score_half = (score_grads * head_scale).astype(jnp.bfloat16)
    query_grads = contract(score_half, keys, 1, 0)
    key_grads = contract(score_half, queries, 0, 0)
    value_grads = contract(probs_half, tangents, 0, 0)
    return outputs, query_grads, key_grads, value_grads


def gather_kernel(index_ref, in_ref, out_ref):
    count = out_ref.shape[0]

    def step(spot, carry):
        out_ref[spot] = in_ref[index_ref[spot]]
        return carry

    lax.fori_loop(0, count, step, 0, unroll=8)


def gather_chunks(index, chunks, count):
    return pl.pallas_call(
        gather_kernel,
        out_shape=jax.ShapeDtypeStruct((count,) + chunks.shape[1:], chunks.dtype),
        in_specs=[
            pl.BlockSpec(memory_space=pltpu.SMEM),
            pl.BlockSpec(memory_space=pltpu.VMEM),
        ],
        out_specs=pl.BlockSpec(memory_space=pltpu.VMEM),
        cost_estimate=pl.CostEstimate(flops=0, bytes_accessed=4 << 20, transcendentals=0),
        name="gather_chunks",
    )(index, chunks)


def cluster_kernel(first_ref, data_ref, out_ref, key_buf, query_sums, key_sums, value_sums):
    key_sums[...] = jnp.zeros_like(key_sums)
    value_sums[...] = jnp.zeros_like(value_sums)

    def make_keys(slot, carry):
        rows = pl.ds(pl.multiple_of(slot * BLOCK, BLOCK), BLOCK)
        floats = data_ref[rows, :HEAD].astype(jnp.float32)
        key_buf[rows, :] = (floats * unit_factor(floats)).astype(jnp.bfloat16)
        return carry

    lax.fori_loop(0, SLOTS, make_keys, 0)

    def visit(slot, first, reach):
        width = reach * BLOCK
        begin = jnp.maximum(slot - (reach - 1), 0)
        rows = pl.ds(pl.multiple_of(slot * BLOCK, BLOCK), BLOCK)
        span = pl.ds(pl.multiple_of(begin * BLOCK, BLOCK), width)
        spot = lax.broadcasted_iota(jnp.int32, (BLOCK, width), 1)
        row = lax.broadcasted_iota(jnp.int32, (BLOCK, width), 0) + (slot - begin) * BLOCK
        self_spot = spot == row
        allowed = (spot <= row) & (spot >= (first - begin) * BLOCK)
        outputs, query_grads, key_grads, value_grads = attend(
            data_ref[rows, :HEAD],
            key_buf[span, :],
            data_ref[span, HEAD : 2 * HEAD],
            data_ref[rows, 2 * HEAD :],
            allowed,
            self_spot,
        )
        out_ref[rows, :HEAD] = outputs.astype(jnp.bfloat16)
        query_sums[rows, :] = query_grads
        key_sums[span, :] += key_grads
        value_sums[span, :] += value_grads

    def step(slot, carry):
        first = first_ref[slot]
        count = slot - first + 1

        @pl.when((first >= 0) & (count <= 2))
        def _():
            visit(slot, first, 2)

        @pl.when((first >= 0) & (count > 2) & (count <= 4))
        def _():
            visit(slot, first, 4)

        @pl.when((first >= 0) & (count > 4))
        def _():
            visit(slot, first, MOST)

        return carry

    lax.fori_loop(0, SLOTS, step, 0)

    def finish(slot, carry):
        rows = pl.ds(pl.multiple_of(slot * BLOCK, BLOCK), BLOCK)
        floats = data_ref[rows, :HEAD].astype(jnp.float32)
        total = query_sums[rows, :] + chain(floats, key_sums[rows, :])
        out_ref[rows, HEAD : 2 * HEAD] = total.astype(jnp.bfloat16)
        out_ref[rows, 2 * HEAD :] = value_sums[rows, :].astype(jnp.bfloat16)
        return carry

    lax.fori_loop(0, SLOTS, finish, 0)


def cluster_attention(first, data):
    rows = data.shape[0]
    return pl.pallas_call(
        cluster_kernel,
        out_shape=jax.ShapeDtypeStruct(data.shape, jnp.bfloat16),
        in_specs=[
            pl.BlockSpec(memory_space=pltpu.SMEM),
            pl.BlockSpec(memory_space=pltpu.VMEM),
        ],
        out_specs=pl.BlockSpec(memory_space=pltpu.VMEM),
        scratch_shapes=[
            pltpu.VMEM((rows, HEAD), jnp.bfloat16),
            pltpu.VMEM((rows, HEAD), jnp.float32),
            pltpu.VMEM((rows, HEAD), jnp.float32),
            pltpu.VMEM((rows, HEAD), jnp.float32),
        ],
        cost_estimate=pl.CostEstimate(
            flops=12 << 30, bytes_accessed=4 << 20, transcendentals=1 << 20
        ),
        name="cluster_attention",
    )(first, data)


def band_kernel(place_ref, data_ref, before_ref, after_ref, out_ref, ext, key_buf, query_sums, key_sums, value_sums):
    own = data_ref.shape[0]
    tiles = own // TILE
    ext[:WINDOW, :] = before_ref[...]
    ext[WINDOW : WINDOW + own, :] = data_ref[...]
    ext[WINDOW + own :, :] = after_ref[...]
    key_sums[...] = jnp.zeros_like(key_sums)
    value_sums[...] = jnp.zeros_like(value_sums)

    def make_keys(tile, carry):
        rows = pl.ds(pl.multiple_of(tile * TILE, TILE), TILE)
        floats = ext[rows, :HEAD].astype(jnp.float32)
        key_buf[rows, :] = (floats * unit_factor(floats)).astype(jnp.bfloat16)
        return carry

    lax.fori_loop(0, tiles + 2, make_keys, 0)
    spot = lax.broadcasted_iota(jnp.int32, (TILE, TILE + WINDOW), 1)
    row = lax.broadcasted_iota(jnp.int32, (TILE, TILE + WINDOW), 0)

    def step(tile, carry):
        rows = pl.ds(pl.multiple_of(tile * TILE + WINDOW, TILE), TILE)
        span = pl.ds(pl.multiple_of(tile * TILE, TILE), TILE + WINDOW)
        least = jnp.where((tile == 0) & (place_ref[0] == 0), WINDOW, 0)
        self_spot = spot == row + WINDOW
        allowed = (spot >= row) & (spot <= row + WINDOW) & (spot >= least)
        outputs, query_grads, key_grads, value_grads = attend(
            ext[rows, :HEAD],
            key_buf[span, :],
            ext[span, HEAD : 2 * HEAD],
            ext[rows, 2 * HEAD :],
            allowed,
            self_spot,
        )
        query_sums[rows, :] = query_grads
        key_sums[span, :] += key_grads
        value_sums[span, :] += value_grads

        @pl.when(tile < tiles)
        def _():
            into = pl.ds(pl.multiple_of(tile * TILE, TILE), TILE)
            out_ref[into, :HEAD] = outputs.astype(jnp.bfloat16)

        return carry

    lax.fori_loop(0, jnp.where(place_ref[1] == 1, tiles, tiles + 1), step, 0)

    def finish(tile, carry):
        rows = pl.ds(pl.multiple_of(tile * TILE + WINDOW, TILE), TILE)
        into = pl.ds(pl.multiple_of(tile * TILE, TILE), TILE)
        floats = ext[rows, :HEAD].astype(jnp.float32)
        total = query_sums[rows, :] + chain(floats, key_sums[rows, :])
        out_ref[into, HEAD : 2 * HEAD] = total.astype(jnp.bfloat16)
        out_ref[into, 2 * HEAD :] = value_sums[rows, :].astype(jnp.bfloat16)
        return carry

    lax.fori_loop(0, tiles, finish, 0)


def band_attention(place, data, before, after):
    rows = data.shape[0] + 2 * WINDOW
    return pl.pallas_call(
        band_kernel,
        out_shape=jax.ShapeDtypeStruct(data.shape, jnp.bfloat16),
        in_specs=[pl.BlockSpec(memory_space=pltpu.SMEM)] + [pl.BlockSpec(memory_space=pltpu.VMEM)] * 3,
        out_specs=pl.BlockSpec(memory_space=pltpu.VMEM),
        scratch_shapes=[
            pltpu.VMEM((rows, 3 * HEAD), jnp.bfloat16),
            pltpu.VMEM((rows, HEAD), jnp.bfloat16),
            pltpu.VMEM((rows, HEAD), jnp.float32),
            pltpu.VMEM((rows, HEAD), jnp.float32),
            pltpu.VMEM((rows, HEAD), jnp.float32),
        ],
        cost_estimate=pl.CostEstimate(
            flops=12 << 30, bytes_accessed=4 << 20, transcendentals=1 << 20
        ),
        name="band_attention",
    )(place, data, before, after)


def shifted(value, axis, steps):
    count = lax.axis_size(axis)
    pairs = [(i, i + steps) for i in range(count) if 0 <= i + steps < count]
    return lax.ppermute(value, axis, pairs)


def turned(value, axis, steps):
    count = lax.axis_size(axis)
    return lax.ppermute(value, axis, [(i, (i + steps) % count) for i in range(count)])


def ring_gather(value, axis):
    half = value.shape[0] // 2
    left = turned(value, axis, 1)
    right = turned(value, axis, -1)
    far_top = turned(left[:half], axis, 1)
    far_low = turned(right[half:], axis, -1)
    far = jnp.concatenate([far_top, far_low], axis=0)
    return value, left, right, far


def exchange(value, axis):
    return lax.all_to_all(value, axis, split_axis=0, concat_axis=0, tiled=True)


def route(labels, seq_count, per_device):
    order = jnp.arange(labels.shape[0], dtype=jnp.int32)
    same = labels[None, :] == labels[:, None]
    rank = jnp.sum(same & (order[None, :] < order[:, None]), axis=1).astype(jnp.int32)
    size = jnp.sum(same, axis=1).astype(jnp.int32)
    rating = size * 4096 - labels
    start = jnp.sum(rating[None, :] > rating[:, None], axis=1).astype(jnp.int32)
    owner = start // per_device
    base = jnp.min(
        jnp.where(owner[None, :] == owner[:, None], start[None, :], labels.shape[0]), axis=1
    ).astype(jnp.int32)
    target = owner * SLOTS + start + rank - base
    head = owner * SLOTS + start - base
    spots = jnp.arange(seq_count * SLOTS, dtype=jnp.int32)
    hits = target[None, :] == spots[:, None]
    picked = jnp.sum(jnp.where(hits, order[None, :], 0), axis=1).astype(jnp.int32)
    first = jnp.sum(jnp.where(hits, head[None, :] % SLOTS + 1, 0), axis=1).astype(jnp.int32) - 1
    return target, picked, first


def on_device(tokens, shared_weight, value_weight, output_weight, cotangent, block_clusters):
    seq_count = lax.axis_size("seq")
    wide_count = lax.axis_size("wide")
    position = lax.axis_index("seq")
    here = lax.axis_index("wide")
    token_count, width = tokens.shape
    block_count = token_count // BLOCK
    piece = BLOCK // seq_count

    routed_pair = jnp.concatenate([shared_weight[:, HEAD:], value_weight[:, HEAD:]], axis=1)
    routed = jnp.concatenate(
        [contract(tokens, routed_pair, 1, 0), contract(cotangent, output_weight[HEAD:], 1, 1)],
        axis=1,
    ).astype(jnp.bfloat16)
    leaving = routed.reshape(block_count, seq_count, piece, 3 * HEAD).transpose(1, 0, 2, 3)
    labels = lax.all_gather(block_clusters[0], "seq", axis=0, tiled=True)
    target, picked, first = route(labels, seq_count, block_count)
    middle = exchange(leaving, "seq").reshape(seq_count * block_count, piece, 3 * HEAD)
    sent = gather_chunks(picked, middle, seq_count * SLOTS)
    arrived = exchange(sent.reshape(seq_count, SLOTS, piece, 3 * HEAD), "seq")
    held = arrived.transpose(1, 0, 2, 3).reshape(SLOTS * BLOCK, 3 * HEAD)
    own_first = lax.dynamic_slice_in_dim(first, position * SLOTS, SLOTS, 0)
    results = cluster_attention(own_first, held)
    turned_back = results.reshape(SLOTS, seq_count, piece, 3 * HEAD).transpose(1, 0, 2, 3)
    middle_back = exchange(turned_back, "seq").reshape(seq_count * SLOTS, piece, 3 * HEAD)
    homeward = gather_chunks(target, middle_back, seq_count * block_count)
    home = exchange(homeward.reshape(seq_count, block_count, piece, 3 * HEAD), "seq")
    routed_all = home.transpose(1, 0, 2, 3).reshape(token_count, 3 * HEAD)

    local_pair = jnp.concatenate([shared_weight[:, :HEAD], value_weight[:, :HEAD]], axis=1)
    local = jnp.concatenate(
        [contract(tokens, local_pair, 1, 0), contract(cotangent, output_weight[:HEAD], 1, 1)],
        axis=1,
    ).astype(jnp.bfloat16)
    before = shifted(local[token_count - WINDOW :], "seq", 1)
    after = shifted(local[:WINDOW], "seq", -1)
    place = jnp.stack([position, (position == seq_count - 1).astype(jnp.int32)])
    local_all = band_attention(place, local, before, after)

    weights = jnp.concatenate([shared_weight, value_weight], axis=1)
    pieces = weights.reshape(wide_count, width // wide_count, weights.shape[1])
    columns = exchange(pieces, "wide")

    def input_part(grads, offset):
        total = None
        for steps, part in zip((0, 1, -1, 2), ring_gather(grads, "wide")):
            owner = (here - steps) % wide_count
            rows = lax.dynamic_slice_in_dim(columns, owner, 1, 0)[0]
            rows = jnp.concatenate(
                [rows[:, offset : offset + HEAD], rows[:, 2 * HEAD + offset : 3 * HEAD + offset]],
                axis=1,
            )
            term = contract(part, rows, 1, 1)
            total = term if total is None else total + term
        return total

    grad_scale = 1.0 / math.sqrt(seq_count * token_count)

    def weight_part(rows):
        terms = jnp.concatenate(
            [contract(tokens, rows[:, HEAD:], 0, 0), contract(cotangent, rows[:, :HEAD], 0, 0)],
            axis=1,
        )
        terms = (terms * grad_scale).astype(jnp.bfloat16)
        terms = exchange(terms.reshape(seq_count, width // seq_count, 3 * HEAD), "seq")
        return jnp.sum(terms.astype(jnp.float32), axis=0)

    local_weights = weight_part(local_all)
    routed_weights = weight_part(routed_all)
    token_grads = (
        input_part(local_all[:, HEAD:], 0) + input_part(routed_all[:, HEAD:], HEAD)
    ).astype(jnp.bfloat16)

    def paired(low, high):
        return jnp.concatenate(
            [local_weights[:, low:high], routed_weights[:, low:high]], axis=1
        )

    return (
        token_grads,
        paired(0, HEAD),
        paired(HEAD, 2 * HEAD),
        paired(2 * HEAD, 3 * HEAD).T,
    )


def solution(mesh):
    placed = (
        P("seq", None),
        P(None, "wide"),
        P(None, "wide"),
        P("wide", None),
        P("seq", None),
        P("wide", "seq"),
    )
    return jax.shard_map(
        on_device,
        mesh=mesh,
        in_specs=placed,
        out_specs=(P("seq", "wide"), P("seq", "wide"), P("seq", "wide"), P("wide", "seq")),
        check_vma=False,
    )
```

```python
import functools
import math

import jax
import jax.numpy as jnp
from jax import lax
from jax.experimental import pallas as pl
from jax.experimental.pallas import tpu as pltpu
from jax.sharding import PartitionSpec as P

HEAD = 128
WINDOW = 256
BLOCK = 128
MOST = 8
SLOTS = 16

EPSILON = 1e-06
NEGATIVE = -1e30
TILE = 256


def contract(left_side, right_side, left_dim, right_dim):
    return lax.dot_general(
        left_side,
        right_side,
        (((left_dim,), (right_dim,)), ((), ())),
        preferred_element_type=jnp.float32,
    )


def unit_factor(floats):
    return lax.rsqrt(jnp.mean(floats * floats, axis=-1, keepdims=True) + EPSILON)


def chain(floats, key_grads):
    factor = unit_factor(floats)
    inner_sum = jnp.sum(floats * key_grads, axis=-1, keepdims=True)
    return factor * key_grads - factor**3 / HEAD * floats * inner_sum


def attend(queries, keys, values, tangents, allowed, self_spot):
    head_scale = 1.0 / math.sqrt(HEAD)
    scores = contract(queries, keys, 1, 1) * head_scale
    scores = jnp.where(self_spot, 0.0, scores)
    scores = jnp.where(allowed, scores, NEGATIVE)
    highest = jnp.max(scores, axis=1, keepdims=True)
    weights = jnp.exp(scores - highest)
    probs = weights * (1.0 / jnp.sum(weights, axis=1, keepdims=True))
    probs_half = probs.astype(jnp.bfloat16)
    outputs = contract(probs_half, values, 1, 0)
    prob_grads = contract(tangents, values, 1, 1)
    centre = jnp.sum(probs * prob_grads, axis=1, keepdims=True)
    score_grads = jnp.where(self_spot, 0.0, probs * (prob_grads - centre))
    score_half = (score_grads * head_scale).astype(jnp.bfloat16)
    query_grads = contract(score_half, keys, 1, 0)
    key_grads = contract(score_half, queries, 0, 0)
    value_grads = contract(probs_half, tangents, 0, 0)
    return outputs, query_grads, key_grads, value_grads


def gather_kernel(index_ref, in_ref, out_ref):
    count = out_ref.shape[0]

    def step(spot, carry):
        out_ref[spot] = in_ref[index_ref[spot]]
        return carry

    lax.fori_loop(0, count, step, 0, unroll=8)


def gather_chunks(index, chunks, count):
    return pl.pallas_call(
        gather_kernel,
        out_shape=jax.ShapeDtypeStruct((count,) + chunks.shape[1:], chunks.dtype),
        in_specs=[
            pl.BlockSpec(memory_space=pltpu.SMEM),
            pl.BlockSpec(memory_space=pltpu.VMEM),
        ],
        out_specs=pl.BlockSpec(memory_space=pltpu.VMEM),
        cost_estimate=pl.CostEstimate(flops=0, bytes_accessed=4 << 20, transcendentals=0),
        name="gather_chunks",
    )(index, chunks)


def cluster_kernel(first_ref, chunk_ref, out_ref, data_ref, key_buf, query_sums, key_sums, value_sums, forward):
    key_sums[...] = jnp.zeros_like(key_sums)
    value_sums[...] = jnp.zeros_like(value_sums)

    def make_keys(slot, carry):
        rows = pl.ds(pl.multiple_of(slot * BLOCK, BLOCK), BLOCK)
        data_ref[rows, :] = chunk_ref[:, slot].reshape(BLOCK, 3 * HEAD)
        floats = data_ref[rows, :HEAD].astype(jnp.float32)
        key_buf[rows, :] = (floats * unit_factor(floats)).astype(jnp.bfloat16)
        return carry

    lax.fori_loop(0, SLOTS, make_keys, 0)

    def visit(slot, first, reach):
        width = reach * BLOCK
        begin = jnp.maximum(slot - (reach - 1), 0)
        rows = pl.ds(pl.multiple_of(slot * BLOCK, BLOCK), BLOCK)
        span = pl.ds(pl.multiple_of(begin * BLOCK, BLOCK), width)
        spot = lax.broadcasted_iota(jnp.int32, (BLOCK, width), 1)
        row = lax.broadcasted_iota(jnp.int32, (BLOCK, width), 0) + (slot - begin) * BLOCK
        self_spot = spot == row
        allowed = (spot <= row) & (spot >= (first - begin) * BLOCK)
        outputs, query_grads, key_grads, value_grads = attend(
            data_ref[rows, :HEAD],
            key_buf[span, :],
            data_ref[span, HEAD : 2 * HEAD],
            data_ref[rows, 2 * HEAD :],
            allowed,
            self_spot,
        )
        forward[rows, :] = outputs.astype(jnp.bfloat16)
        query_sums[rows, :] = query_grads
        key_sums[span, :] += key_grads
        value_sums[span, :] += value_grads

    def step(slot, carry):
        first = first_ref[slot]
        count = slot - first + 1

        @pl.when((first >= 0) & (count <= 2))
        def _():
            visit(slot, first, 2)

        @pl.when((first >= 0) & (count > 2) & (count <= 4))
        def _():
            visit(slot, first, 4)

        @pl.when((first >= 0) & (count > 4))
        def _():
            visit(slot, first, MOST)

        return carry

    lax.fori_loop(0, SLOTS, step, 0)

    def finish(slot, carry):
        rows = pl.ds(pl.multiple_of(slot * BLOCK, BLOCK), BLOCK)
        floats = data_ref[rows, :HEAD].astype(jnp.float32)
        total = query_sums[rows, :] + chain(floats, key_sums[rows, :])
        joined = jnp.concatenate(
            [
                forward[rows, :],
                total.astype(jnp.bfloat16),
                value_sums[rows, :].astype(jnp.bfloat16),
            ],
            axis=1,
        )
        out_ref[:, slot] = joined.reshape(chunk_ref.shape[0], chunk_ref.shape[2], 3 * HEAD)
        return carry

    lax.fori_loop(0, SLOTS, finish, 0)


def cluster_attention(first, data):
    rows = SLOTS * BLOCK
    return pl.pallas_call(
        cluster_kernel,
        out_shape=jax.ShapeDtypeStruct(data.shape, jnp.bfloat16),
        in_specs=[
            pl.BlockSpec(memory_space=pltpu.SMEM),
            pl.BlockSpec(memory_space=pltpu.VMEM),
        ],
        out_specs=pl.BlockSpec(memory_space=pltpu.VMEM),
        scratch_shapes=[
            pltpu.VMEM((rows, 3 * HEAD), jnp.bfloat16),
            pltpu.VMEM((rows, HEAD), jnp.bfloat16),
            pltpu.VMEM((rows, HEAD), jnp.float32),
            pltpu.VMEM((rows, HEAD), jnp.float32),
            pltpu.VMEM((rows, HEAD), jnp.float32),
            pltpu.VMEM((rows, HEAD), jnp.bfloat16),
        ],
        cost_estimate=pl.CostEstimate(
            flops=12 << 30, bytes_accessed=4 << 20, transcendentals=1 << 20
        ),
        name="cluster_attention",
    )(first, data)


def band_kernel(place_ref, data_ref, before_ref, after_ref, out_ref, ext, key_buf, query_sums, key_sums, value_sums):
    own = data_ref.shape[0]
    tiles = own // TILE
    ext[:WINDOW, :] = before_ref[...]
    ext[WINDOW : WINDOW + own, :] = data_ref[...]
    ext[WINDOW + own :, :] = after_ref[...]
    key_sums[...] = jnp.zeros_like(key_sums)
    value_sums[...] = jnp.zeros_like(value_sums)

    def make_keys(tile, carry):
        rows = pl.ds(pl.multiple_of(tile * TILE, TILE), TILE)
        floats = ext[rows, :HEAD].astype(jnp.float32)
        key_buf[rows, :] = (floats * unit_factor(floats)).astype(jnp.bfloat16)
        return carry

    lax.fori_loop(0, tiles + 2, make_keys, 0)
    spot = lax.broadcasted_iota(jnp.int32, (TILE, TILE + WINDOW), 1)
    row = lax.broadcasted_iota(jnp.int32, (TILE, TILE + WINDOW), 0)

    def step(tile, carry):
        rows = pl.ds(pl.multiple_of(tile * TILE + WINDOW, TILE), TILE)
        span = pl.ds(pl.multiple_of(tile * TILE, TILE), TILE + WINDOW)
        least = jnp.where((tile == 0) & (place_ref[0] == 0), WINDOW, 0)
        self_spot = spot == row + WINDOW
        allowed = (spot >= row) & (spot <= row + WINDOW) & (spot >= least)
        outputs, query_grads, key_grads, value_grads = attend(
            ext[rows, :HEAD],
            key_buf[span, :],
            ext[span, HEAD : 2 * HEAD],
            ext[rows, 2 * HEAD :],
            allowed,
            self_spot,
        )
        query_sums[rows, :] = query_grads
        key_sums[span, :] += key_grads
        value_sums[span, :] += value_grads

        @pl.when(tile < tiles)
        def _():
            into = pl.ds(pl.multiple_of(tile * TILE, TILE), TILE)
            out_ref[into, :HEAD] = outputs.astype(jnp.bfloat16)

        return carry

    lax.fori_loop(0, jnp.where(place_ref[1] == 1, tiles, tiles + 1), step, 0)

    def finish(tile, carry):
        rows = pl.ds(pl.multiple_of(tile * TILE + WINDOW, TILE), TILE)
        into = pl.ds(pl.multiple_of(tile * TILE, TILE), TILE)
        floats = ext[rows, :HEAD].astype(jnp.float32)
        total = query_sums[rows, :] + chain(floats, key_sums[rows, :])
        out_ref[into, HEAD : 2 * HEAD] = total.astype(jnp.bfloat16)
        out_ref[into, 2 * HEAD :] = value_sums[rows, :].astype(jnp.bfloat16)
        return carry

    lax.fori_loop(0, tiles, finish, 0)


def band_attention(place, data, before, after):
    rows = data.shape[0] + 2 * WINDOW
    return pl.pallas_call(
        band_kernel,
        out_shape=jax.ShapeDtypeStruct(data.shape, jnp.bfloat16),
        in_specs=[pl.BlockSpec(memory_space=pltpu.SMEM)] + [pl.BlockSpec(memory_space=pltpu.VMEM)] * 3,
        out_specs=pl.BlockSpec(memory_space=pltpu.VMEM),
        scratch_shapes=[
            pltpu.VMEM((rows, 3 * HEAD), jnp.bfloat16),
            pltpu.VMEM((rows, HEAD), jnp.bfloat16),
            pltpu.VMEM((rows, HEAD), jnp.float32),
            pltpu.VMEM((rows, HEAD), jnp.float32),
            pltpu.VMEM((rows, HEAD), jnp.float32),
        ],
        cost_estimate=pl.CostEstimate(
            flops=12 << 30, bytes_accessed=4 << 20, transcendentals=1 << 20
        ),
        name="band_attention",
    )(place, data, before, after)


def shifted(value, axis, steps):
    count = lax.axis_size(axis)
    pairs = [(i, i + steps) for i in range(count) if 0 <= i + steps < count]
    return lax.ppermute(value, axis, pairs)


def turned(value, axis, steps):
    count = lax.axis_size(axis)
    return lax.ppermute(value, axis, [(i, (i + steps) % count) for i in range(count)])


def exchange(value, axis):
    return lax.all_to_all(value, axis, split_axis=0, concat_axis=0, tiled=True)


def route(labels, seq_count, per_device):
    order = jnp.arange(labels.shape[0], dtype=jnp.int32)
    same = labels[None, :] == labels[:, None]
    rank = jnp.sum(same & (order[None, :] < order[:, None]), axis=1).astype(jnp.int32)
    size = jnp.sum(same, axis=1).astype(jnp.int32)
    rating = size * 4096 - labels
    start = jnp.sum(rating[None, :] > rating[:, None], axis=1).astype(jnp.int32)
    owner = start // per_device
    base = jnp.min(
        jnp.where(owner[None, :] == owner[:, None], start[None, :], labels.shape[0]), axis=1
    ).astype(jnp.int32)
    target = owner * SLOTS + start + rank - base
    head = owner * SLOTS + start - base
    spots = jnp.arange(seq_count * SLOTS, dtype=jnp.int32)
    hits = target[None, :] == spots[:, None]
    picked = jnp.sum(jnp.where(hits, order[None, :], 0), axis=1).astype(jnp.int32)
    first = jnp.sum(jnp.where(hits, head[None, :] % SLOTS + 1, 0), axis=1).astype(jnp.int32) - 1
    return target, picked, first


def project_kernel(tokens_ref, shared_ref, value_ref, cotangent_ref, output_ref, out_ref):
    tokens = tokens_ref[...]
    joined = jnp.concatenate(
        [
            contract(tokens, shared_ref[...], 1, 0),
            contract(tokens, value_ref[...], 1, 0),
            contract(cotangent_ref[...], output_ref[...], 1, 1),
        ],
        axis=1,
    ).astype(jnp.bfloat16)
    if len(out_ref.shape) == 2:
        out_ref[...] = joined
        return
    for slot in range(out_ref.shape[1]):
        out_ref[:, slot] = joined[slot * BLOCK : (slot + 1) * BLOCK].reshape(
            out_ref.shape[0], out_ref.shape[2], 3 * HEAD
        )


def project(tokens, shared_weight, value_weight, cotangent, output_weight, head, parts):
    token_count, width = tokens.shape
    if parts:
        piece = BLOCK // parts
        shape = (parts, token_count // BLOCK, piece, 3 * HEAD)
        spec = pl.BlockSpec((parts, TILE // BLOCK, piece, 3 * HEAD), lambda i: (0, i, 0, 0))
    else:
        shape = (token_count, 3 * HEAD)
        spec = pl.BlockSpec((TILE, 3 * HEAD), lambda i: (i, 0))
    rows = pl.BlockSpec((TILE, width), lambda i: (i, 0))
    columns = pl.BlockSpec((width, HEAD), lambda i: (0, head))
    return pl.pallas_call(
        project_kernel,
        grid=(token_count // TILE,),
        out_shape=jax.ShapeDtypeStruct(shape, jnp.bfloat16),
        in_specs=[rows, columns, columns, rows, pl.BlockSpec((HEAD, width), lambda i: (head, 0))],
        out_specs=spec,
        cost_estimate=pl.CostEstimate(
            flops=6 * token_count * width * HEAD, bytes_accessed=8 << 20, transcendentals=0
        ),
        name="project",
    )(tokens, shared_weight, value_weight, cotangent, output_weight)


def weight_terms(turned_rows, tokens_ref, cotangent_ref, scale, store):
    def step(part, carry):
        span = pl.ds(pl.multiple_of(part * TILE, TILE), TILE)
        terms = jnp.concatenate(
            [
                contract(turned_rows[HEAD:, :], tokens_ref[:, span], 1, 0),
                contract(turned_rows[:HEAD, :], cotangent_ref[:, span], 1, 0),
            ],
            axis=0,
        )
        store(part, (terms * scale).T.astype(jnp.bfloat16))
        return carry

    lax.fori_loop(0, tokens_ref.shape[1] // TILE, step, 0)


def local_terms_kernel(scale, rows_ref, tokens_ref, cotangent_ref, out_ref, turned_rows):
    turned_rows[...] = rows_ref[...].T

    def store(part, terms):
        out_ref[pl.ds(pl.multiple_of(part * TILE, TILE), TILE), :] = terms

    weight_terms(turned_rows, tokens_ref, cotangent_ref, scale, store)


def local_terms(rows, tokens, cotangent, scale):
    count, width = tokens.shape
    return pl.pallas_call(
        functools.partial(local_terms_kernel, scale),
        out_shape=jax.ShapeDtypeStruct((width, 3 * HEAD), jnp.bfloat16),
        in_specs=[pl.BlockSpec(memory_space=pltpu.VMEM)] * 3,
        out_specs=pl.BlockSpec(memory_space=pltpu.VMEM),
        scratch_shapes=[pltpu.VMEM((3 * HEAD, count), jnp.bfloat16)],
        cost_estimate=pl.CostEstimate(
            flops=6 * count * width * HEAD, bytes_accessed=8 << 20, transcendentals=0
        ),
        name="local_terms",
    )(rows, tokens, cotangent)


MESH = pl.DeviceIdType.MESH


def final_kernel(
    seq_count,
    wide_count,
    scale,
    home,
    tokens_hbm,
    cotangent_hbm,
    local_ref,
    part_ref,
    columns,
    token_out,
    shared_out,
    value_out,
    output_out,
    tokens_buf,
    cotangent_buf,
    rows_buf,
    turned_rows,
    from_left,
    from_right,
    from_far,
    total,
    pieces,
    arrived,
    load_sem,
    send_sem,
    recv_sem,
    piece_send,
    piece_recv,
):
    me = lax.axis_index("seq")
    here = lax.axis_index("wide")
    right = lax.rem(here + 1, wide_count)
    left = lax.rem(here + wide_count - 1, wide_count)
    far = lax.rem(here + 2, wide_count)
    chunks, slots, piece = home.shape[:3]
    half = chunks // 2
    tops = pl.ds(0, half)
    lows = pl.ds(half, half)
    grads = pl.ds(HEAD, 2 * HEAD)

    load_tokens = pltpu.make_async_copy(tokens_hbm, tokens_buf, load_sem.at[0])
    load_cotangent = pltpu.make_async_copy(cotangent_hbm, cotangent_buf, load_sem.at[1])
    load_tokens.start()
    load_cotangent.start()

    barrier = pltpu.get_barrier_semaphore()
    for side in (left, right):
        pl.semaphore_signal(barrier, inc=1, device_id={"wide": side}, device_id_type=MESH)

    def greet(step, carry):
        peer = lax.rem(me + step, seq_count)
        pl.semaphore_signal(barrier, inc=1, device_id={"seq": peer}, device_id_type=MESH)
        return carry

    lax.fori_loop(1, seq_count, greet, 0)
    pl.semaphore_wait(barrier, seq_count + 1)

    def sending(source, target, number, side):
        return pltpu.make_async_remote_copy(
            src_ref=source,
            dst_ref=target,
            send_sem=send_sem.at[number],
            recv_sem=recv_sem.at[number],
            device_id={"wide": side},
            device_id_type=MESH,
        )

    right_top = sending(home.at[tops, :, :, grads], from_left.at[tops], 0, right)
    right_low = sending(home.at[lows, :, :, grads], from_left.at[lows], 1, right)
    left_top = sending(home.at[tops, :, :, grads], from_right.at[tops], 2, left)
    left_low = sending(home.at[lows, :, :, grads], from_right.at[lows], 3, left)
    onward_top = sending(from_left.at[tops], from_far.at[tops], 4, right)
    onward_low = sending(from_right.at[lows], from_far.at[lows], 5, left)
    right_top.start()
    left_low.start()
    right_low.start()
    left_top.start()

    def merge(slot, carry):
        span = pl.ds(pl.multiple_of(slot * BLOCK, BLOCK), BLOCK)
        rows = home[:, slot].reshape(BLOCK, 3 * HEAD)
        rows_buf[span, :] = rows
        turned_rows[:, span] = rows.T
        return carry

    lax.fori_loop(0, slots, merge, 0)
    load_tokens.wait()
    load_cotangent.wait()
    share = home.shape[0]
    rows_each = pieces.shape[1]
    per_part = TILE // rows_each

    def store(part, terms):
        pieces[pl.ds(part * per_part, per_part), :, 3 * HEAD :] = terms.reshape(
            per_part, rows_each, 3 * HEAD
        )

    pieces[:, :, : 3 * HEAD] = local_ref[...]
    weight_terms(turned_rows, tokens_buf, cotangent_buf, scale, store)

    def piece_copy(peer, slot):
        return pltpu.make_async_remote_copy(
            src_ref=pieces.at[peer],
            dst_ref=arrived.at[slot],
            send_sem=piece_send.at[peer],
            recv_sem=piece_recv.at[slot],
            device_id={"seq": peer},
            device_id_type=MESH,
        )

    def send_piece(step, carry):
        piece_copy(lax.rem(me + step, seq_count), me).start()
        return carry

    lax.fori_loop(1, seq_count, send_piece, 0)

    def add_terms(source, owner, first, last):
        weights = columns[owner]

        def step(slot, carry):
            span = pl.ds(pl.multiple_of(slot * BLOCK, BLOCK), BLOCK)
            rows = source(slot, span)
            base = part_ref[span, :] if first else total[span, :]
            value = base + contract(rows, weights, 1, 1)
            if last:
                token_out[span, :] = value.astype(jnp.bfloat16)
            else:
                total[span, :] = value
            return carry

        lax.fori_loop(0, slots, step, 0)

    def merged(buffer):
        return lambda slot, span: buffer[:, slot].reshape(BLOCK, 2 * HEAD)

    right_top.wait_recv()
    onward_top.start()
    left_low.wait_recv()
    onward_low.start()
    add_terms(lambda slot, span: rows_buf[span, HEAD:], here, True, False)
    right_low.wait_recv()
    add_terms(merged(from_left), left, False, False)
    left_top.wait_recv()
    add_terms(merged(from_right), right, False, False)
    onward_top.wait_recv()
    onward_low.wait_recv()
    add_terms(merged(from_far), far, False, True)

    def take(step, sums):
        peer = lax.rem(me + step, seq_count)
        piece_copy(peer, peer).wait_recv()
        return sums + arrived[peer].astype(jnp.float32)

    sums = lax.fori_loop(1, seq_count, take, pieces[me].astype(jnp.float32))

    def paired(number):
        low = number * HEAD
        return jnp.concatenate(
            [sums[:, low : low + HEAD], sums[:, 3 * HEAD + low : 4 * HEAD + low]], axis=1
        )

    shared_out[...] = paired(0)
    value_out[...] = paired(1)
    output_out[...] = paired(2)

    for copy in (right_top, right_low, left_top, left_low, onward_top, onward_low):
        copy.wait_send()

    def drain(step, carry):
        peer = lax.rem(me + step, seq_count)
        piece_copy(peer, me).wait_send()
        return carry

    lax.fori_loop(1, seq_count, drain, 0)


def final_step(home, tokens, cotangent, local_part_terms, part, columns, scale):
    count, width = tokens.shape
    seq_count = lax.axis_size("seq")
    wide_count = lax.axis_size("wide")
    each = width // seq_count
    out_width = width // wide_count
    chunk = home.shape[:3] + (2 * HEAD,)
    vmem = pl.BlockSpec(memory_space=pltpu.VMEM)
    anywhere = pl.BlockSpec(memory_space=pl.ANY)
    small = jax.ShapeDtypeStruct((each, 2 * HEAD), jnp.float32)
    return pl.pallas_call(
        functools.partial(final_kernel, seq_count, wide_count, scale),
        out_shape=(
            jax.ShapeDtypeStruct((count, out_width), jnp.bfloat16),
            small,
            small,
            small,
        ),
        in_specs=[vmem, anywhere, anywhere, vmem, vmem, vmem],
        out_specs=(vmem,) * 4,
        scratch_shapes=[
            pltpu.VMEM((count, width), jnp.bfloat16),
            pltpu.VMEM((count, width), jnp.bfloat16),
            pltpu.VMEM((count, 3 * HEAD), jnp.bfloat16),
            pltpu.VMEM((3 * HEAD, count), jnp.bfloat16),
            pltpu.VMEM(chunk, jnp.bfloat16),
            pltpu.VMEM(chunk, jnp.bfloat16),
            pltpu.VMEM(chunk, jnp.bfloat16),
            pltpu.VMEM((count, out_width), jnp.float32),
            pltpu.VMEM((seq_count, each, 6 * HEAD), jnp.bfloat16),
            pltpu.VMEM((seq_count, each, 6 * HEAD), jnp.bfloat16),
            pltpu.SemaphoreType.DMA((2,)),
            pltpu.SemaphoreType.DMA((6,)),
            pltpu.SemaphoreType.DMA((6,)),
            pltpu.SemaphoreType.DMA((seq_count,)),
            pltpu.SemaphoreType.DMA((seq_count,)),
        ],
        compiler_params=pltpu.CompilerParams(collective_id=0, has_side_effects=True),
        cost_estimate=pl.CostEstimate(
            flops=30 << 30, bytes_accessed=16 << 20, transcendentals=0
        ),
        name="final_step",
    )(home, tokens, cotangent, local_part_terms, part, columns)


def on_device(tokens, shared_weight, value_weight, output_weight, cotangent, block_clusters):
    seq_count = lax.axis_size("seq")
    wide_count = lax.axis_size("wide")
    position = lax.axis_index("seq")
    here = lax.axis_index("wide")
    token_count, width = tokens.shape
    block_count = token_count // BLOCK
    piece = BLOCK // seq_count
    grad_scale = 1.0 / math.sqrt(seq_count * token_count)
    ends = (tokens, shared_weight, value_weight, cotangent, output_weight)

    leaving = project(*ends, 1, seq_count)
    middle = exchange(leaving, "seq").reshape(seq_count * block_count, piece, 3 * HEAD)
    spread = jnp.broadcast_to(block_clusters[None], (seq_count, 1, block_count))
    labels = exchange(spread, "seq").reshape(seq_count * block_count)
    target, picked, first = route(labels, seq_count, block_count)

    local = project(*ends, 0, 0)
    before = shifted(local[token_count - WINDOW :], "seq", 1)
    after = shifted(local[:WINDOW], "seq", -1)
    place = jnp.stack([position, (position == seq_count - 1).astype(jnp.int32)])
    weights = jnp.concatenate(
        [shared_weight[:, :HEAD], value_weight[:, :HEAD], shared_weight[:, HEAD:], value_weight[:, HEAD:]],
        axis=1,
    )
    columns = exchange(weights.reshape(wide_count, width // wide_count, 4 * HEAD), "wide")

    sent = gather_chunks(picked, middle, seq_count * SLOTS)
    sent, local = lax.optimization_barrier((sent, local))
    arrived = exchange(sent.reshape(seq_count, SLOTS, piece, 3 * HEAD), "seq")
    local_all = band_attention(place, local, before, after)

    own_first = lax.dynamic_slice_in_dim(first, position * SLOTS, SLOTS, 0)
    results = cluster_attention(own_first, arrived)
    results, local_all = lax.optimization_barrier((results, local_all))
    middle_back = exchange(results, "seq").reshape(seq_count * SLOTS, piece, 3 * HEAD)
    local_grads = local_all[:, HEAD:]
    local_sides = [turned(local_grads, "wide", steps) for steps in (1, -1, 2)]
    terms = local_terms(local_all, tokens, cotangent, grad_scale)
    homeward = gather_chunks(target, middle_back, seq_count * block_count)
    home = exchange(homeward.reshape(seq_count, block_count, piece, 3 * HEAD), "seq")

    part = None
    for steps, grads in zip((0, 1, -1, 2), [local_grads] + local_sides):
        owner = (here - steps) % wide_count
        rows = lax.dynamic_slice_in_dim(columns, owner, 1, 0)[0, :, : 2 * HEAD]
        term = contract(grads, rows, 1, 1)
        part = term if part is None else part + term

    token_grads, shared_grads, value_grads, output_grads = final_step(
        home,
        tokens,
        cotangent,
        terms.reshape(seq_count, width // seq_count, 3 * HEAD),
        part,
        columns[:, :, 2 * HEAD :],
        grad_scale,
    )
    return token_grads, shared_grads, value_grads, output_grads.T


def solution(mesh):
    placed = (
        P("seq", None),
        P(None, "wide"),
        P(None, "wide"),
        P("wide", None),
        P("seq", None),
        P("wide", "seq"),
    )
    return jax.shard_map(
        on_device,
        mesh=mesh,
        in_specs=placed,
        out_specs=(P("seq", "wide"), P("seq", "wide"), P("seq", "wide"), P("wide", "seq")),
        check_vma=False,
    )
```

```python
import functools
import math

import jax
import jax.numpy as jnp
from jax import lax
from jax.experimental import pallas as pl
from jax.experimental.pallas import tpu as pltpu
from jax.sharding import PartitionSpec as P

HEAD = 128
WINDOW = 256
BLOCK = 128
MOST = 8
SLOTS = 16

EPSILON = 1e-06
NEGATIVE = -1e30
TILE = 256
GROUP = 4
BAND_GROUP = 3


def contract(left_side, right_side, left_dim, right_dim):
    return lax.dot_general(
        left_side,
        right_side,
        (((left_dim,), (right_dim,)), ((), ())),
        preferred_element_type=jnp.float32,
    )


def unit_factor(floats):
    return lax.rsqrt(jnp.mean(floats * floats, axis=-1, keepdims=True) + EPSILON)


def chain(floats, key_grads):
    factor = unit_factor(floats)
    inner_sum = jnp.sum(floats * key_grads, axis=-1, keepdims=True)
    return factor * key_grads - factor**3 / HEAD * floats * inner_sum


SCALE = 1.0 / math.sqrt(HEAD)
POWER = SCALE * math.log2(math.e)


def attend(jobs):
    scores = [mask(contract(q, k, 1, 1)) for q, k, v, t, mask, unself in jobs]
    prob_grads = [contract(t, v, 1, 1) for q, k, v, t, mask, unself in jobs]
    highest = [jnp.max(s, axis=1, keepdims=True) for s in scores]
    weights = [jnp.exp2((s - h) * POWER) for s, h in zip(scores, highest)]
    shares = [1.0 / jnp.sum(w, axis=1, keepdims=True) for w in weights]
    halves = [(w * share).astype(jnp.bfloat16) for w, share in zip(weights, shares)]
    centres = [
        share * jnp.sum(w * g, axis=1, keepdims=True)
        for w, g, share in zip(weights, prob_grads, shares)
    ]
    score_halves = [
        job[5](w * (share * SCALE) * (g - c)).astype(jnp.bfloat16)
        for job, w, share, g, c in zip(jobs, weights, shares, prob_grads, centres)
    ]
    outputs = [contract(h, job[2], 1, 0) for h, job in zip(halves, jobs)]
    query_grads = [contract(h, job[1], 1, 0) for h, job in zip(score_halves, jobs)]
    value_grads = [contract(h, job[3], 0, 0) for h, job in zip(halves, jobs)]
    key_grads = [contract(h, job[0], 0, 0) for h, job in zip(score_halves, jobs)]
    return zip(outputs, query_grads, key_grads, value_grads)


def cluster_kernel(
    first_ref, chunk_ref, out_ref, data_ref, key_buf, query_sums, key_sums, value_sums, forward
):
    pad = (MOST - 1) * BLOCK
    key_sums[...] = jnp.zeros_like(key_sums)
    value_sums[...] = jnp.zeros_like(value_sums)
    data_ref[:pad, :] = jnp.zeros((pad, 3 * HEAD), jnp.bfloat16)
    key_buf[:pad, :] = jnp.zeros((pad, HEAD), jnp.bfloat16)

    def rows_of(slot):
        return pl.ds(pl.multiple_of((slot + MOST - 1) * BLOCK, BLOCK), BLOCK)

    def make_keys(slot, carry):
        rows = rows_of(slot)
        data = chunk_ref[:, slot].reshape(BLOCK, 3 * HEAD)
        data_ref[rows, :] = data
        floats = data[:, :HEAD].astype(jnp.float32)
        key_buf[rows, :] = (floats * unit_factor(floats)).astype(jnp.bfloat16)
        return carry

    lax.fori_loop(0, SLOTS, make_keys, 0, unroll=4)
    spot = lax.broadcasted_iota(jnp.int32, (BLOCK, BLOCK), 1)
    row = lax.broadcasted_iota(jnp.int32, (BLOCK, BLOCK), 0)

    def unself(grads):
        width = grads.shape[1]
        last = jnp.where(spot == row, 0.0, grads[:, width - BLOCK :])
        if width == BLOCK:
            return last
        return jnp.concatenate([grads[:, : width - BLOCK], last], axis=1)

    def visit(begin, counts, reach):
        width = reach * BLOCK
        jobs = []
        for number, count in enumerate(counts):
            rows = rows_of(begin + number)
            span = pl.ds(pl.multiple_of((begin + number + MOST - reach) * BLOCK, BLOCK), width)

            def mask(scores, count=count):
                last = jnp.where(
                    spot < row,
                    scores[:, width - BLOCK :],
                    jnp.where(spot == row, 0.0, NEGATIVE),
                )
                if reach == 1:
                    return last
                place = lax.broadcasted_iota(jnp.int32, (BLOCK, width - BLOCK), 1)
                least = (reach - count) * BLOCK
                rest = jnp.where(place >= least, scores[:, : width - BLOCK], NEGATIVE)
                return jnp.concatenate([rest, last], axis=1)

            jobs.append(
                (
                    data_ref[rows, :HEAD],
                    key_buf[span, :],
                    data_ref[span, HEAD : 2 * HEAD],
                    data_ref[rows, 2 * HEAD :],
                    mask,
                    unself,
                )
            )
        for number, (outputs, query_grads, key_grads, value_grads) in enumerate(attend(jobs)):
            rows = rows_of(begin + number)
            span = pl.ds(pl.multiple_of((begin + number + MOST - reach) * BLOCK, BLOCK), width)
            forward[rows, :] = outputs.astype(jnp.bfloat16)
            query_sums[rows, :] = query_grads
            key_sums[span, :] += key_grads
            value_sums[span, :] += value_grads

    def step(group, carry):
        begin = group * GROUP
        counts = []
        for number in range(GROUP):
            first = first_ref[begin + number]
            counts.append(jnp.where(first >= 0, begin + number - first + 1, 1))
        most = functools.reduce(jnp.maximum, counts)
        for low, reach in ((0, 1), (1, 2), (2, 4), (4, MOST)):

            @pl.when((most > low) & (most <= reach))
            def _(reach=reach):
                visit(begin, counts, reach)

        return carry

    lax.fori_loop(0, SLOTS // GROUP, step, 0)

    def finish(slot, carry):
        rows = rows_of(slot)
        floats = data_ref[rows, :HEAD].astype(jnp.float32)
        total = query_sums[rows, :] + chain(floats, key_sums[rows, :])
        joined = jnp.concatenate(
            [
                forward[rows, :],
                total.astype(jnp.bfloat16),
                value_sums[rows, :].astype(jnp.bfloat16),
            ],
            axis=1,
        )
        out_ref[:, slot] = joined.reshape(chunk_ref.shape[0], chunk_ref.shape[2], 3 * HEAD)
        return carry

    lax.fori_loop(0, SLOTS, finish, 0, unroll=4)


def cluster_attention(first, data):
    rows = (SLOTS + MOST - 1) * BLOCK
    return pl.pallas_call(
        cluster_kernel,
        out_shape=jax.ShapeDtypeStruct(data.shape, jnp.bfloat16),
        in_specs=[
            pl.BlockSpec(memory_space=pltpu.SMEM),
            pl.BlockSpec(memory_space=pltpu.VMEM),
        ],
        out_specs=pl.BlockSpec(memory_space=pltpu.VMEM),
        scratch_shapes=[
            pltpu.VMEM((rows, 3 * HEAD), jnp.bfloat16),
            pltpu.VMEM((rows, HEAD), jnp.bfloat16),
            pltpu.VMEM((rows, HEAD), jnp.float32),
            pltpu.VMEM((rows, HEAD), jnp.float32),
            pltpu.VMEM((rows, HEAD), jnp.float32),
            pltpu.VMEM((rows, HEAD), jnp.bfloat16),
        ],
        cost_estimate=pl.CostEstimate(
            flops=12 << 30, bytes_accessed=4 << 20, transcendentals=1 << 20
        ),
        name="cluster_attention",
    )(first, data)


def band_body(
    is_first, is_last, data_ref, before_ref, after_ref, out_ref, ext, key_buf, query_sums, key_sums, value_sums
):
    own = data_ref.shape[0]
    tiles = own // TILE
    ext[:WINDOW, :] = before_ref[...]
    ext[WINDOW : WINDOW + own, :] = data_ref[...]
    after = after_ref[...]
    ext[WINDOW + own :, :] = jnp.where(is_last, jnp.zeros_like(after), after)
    key_sums[...] = jnp.zeros_like(key_sums)
    value_sums[...] = jnp.zeros_like(value_sums)

    def make_keys(tile, carry):
        rows = pl.ds(pl.multiple_of(tile * TILE, TILE), TILE)
        floats = ext[rows, :HEAD].astype(jnp.float32)
        key_buf[rows, :] = (floats * unit_factor(floats)).astype(jnp.bfloat16)
        return carry

    lax.fori_loop(0, tiles + 2, make_keys, 0, unroll=4)
    spot = lax.broadcasted_iota(jnp.int32, (TILE, TILE), 1)
    row = lax.broadcasted_iota(jnp.int32, (TILE, TILE), 0)

    def unself(grads):
        last = jnp.where(spot == row, 0.0, grads[:, WINDOW:])
        return jnp.concatenate([grads[:, :WINDOW], last], axis=1)

    def mask(scores, tile):
        inside = spot >= row
        if tile == 0:
            inside = inside & (spot >= jnp.where(is_first, WINDOW, 0))
        first = jnp.where(inside, scores[:, :WINDOW], NEGATIVE)
        last = jnp.where(
            spot < row, scores[:, WINDOW:], jnp.where(spot == row, 0.0, NEGATIVE)
        )
        return jnp.concatenate([first, last], axis=1)

    for begin in range(0, tiles + 1, BAND_GROUP):
        group = range(begin, min(begin + BAND_GROUP, tiles + 1))
        jobs = []
        for tile in group:
            rows = pl.ds(tile * TILE + WINDOW, TILE)
            span = pl.ds(tile * TILE, TILE + WINDOW)
            jobs.append(
                (
                    ext[rows, :HEAD],
                    key_buf[span, :],
                    ext[span, HEAD : 2 * HEAD],
                    ext[rows, 2 * HEAD :],
                    functools.partial(mask, tile=tile),
                    unself,
                )
            )
        for tile, (outputs, query_grads, key_grads, value_grads) in zip(group, attend(jobs)):
            rows = pl.ds(tile * TILE + WINDOW, TILE)
            span = pl.ds(tile * TILE, TILE + WINDOW)
            query_sums[rows, :] = query_grads
            key_sums[span, :] += key_grads
            value_sums[span, :] += value_grads
            if tile < tiles:
                out_ref[pl.ds(tile * TILE, TILE), :HEAD] = outputs.astype(jnp.bfloat16)

    def finish(tile, carry):
        rows = pl.ds(pl.multiple_of(tile * TILE + WINDOW, TILE), TILE)
        into = pl.ds(pl.multiple_of(tile * TILE, TILE), TILE)
        floats = ext[rows, :HEAD].astype(jnp.float32)
        total = query_sums[rows, :] + chain(floats, key_sums[rows, :])
        out_ref[into, HEAD : 2 * HEAD] = total.astype(jnp.bfloat16)
        out_ref[into, 2 * HEAD :] = value_sums[rows, :].astype(jnp.bfloat16)
        return carry

    lax.fori_loop(0, tiles, finish, 0, unroll=3)


def route(labels, seq_count, per_device):
    order = jnp.arange(labels.shape[0], dtype=jnp.int32)
    same = labels[None, :] == labels[:, None]
    rank = jnp.sum(same & (order[None, :] < order[:, None]), axis=1).astype(jnp.int32)
    size = jnp.sum(same, axis=1).astype(jnp.int32)
    rating = size * 4096 - labels
    start = jnp.sum(rating[None, :] > rating[:, None], axis=1).astype(jnp.int32)
    owner = start // per_device
    base = jnp.min(
        jnp.where(owner[None, :] == owner[:, None], start[None, :], labels.shape[0]), axis=1
    ).astype(jnp.int32)
    target = owner * SLOTS + start + rank - base
    head = owner * SLOTS + start - base
    spots = jnp.arange(seq_count * SLOTS, dtype=jnp.int32)
    hits = target[None, :] == spots[:, None]
    picked = jnp.sum(jnp.where(hits, order[None, :], 0), axis=1).astype(jnp.int32)
    first = jnp.sum(jnp.where(hits, head[None, :] % SLOTS + 1, 0), axis=1).astype(jnp.int32) - 1
    return target, picked, first


def project_tile(tokens, cotangent, shared_ref, value_ref, output_ref):
    return jnp.concatenate(
        [
            contract(tokens, shared_ref[...], 1, 0),
            contract(tokens, value_ref[...], 1, 0),
            contract(cotangent, output_ref[...], 1, 1),
        ],
        axis=1,
    ).astype(jnp.bfloat16)


def project_kernel(tokens_ref, shared_ref, value_ref, cotangent_ref, output_ref, out_ref):
    joined = project_tile(tokens_ref[...], cotangent_ref[...], shared_ref, value_ref, output_ref)
    for slot in range(out_ref.shape[1]):
        out_ref[:, slot] = joined[slot * BLOCK : (slot + 1) * BLOCK].reshape(
            out_ref.shape[0], out_ref.shape[2], 3 * HEAD
        )


def project(tokens, shared_weight, value_weight, cotangent, output_weight, parts):
    token_count, width = tokens.shape
    piece = BLOCK // parts
    rows = pl.BlockSpec((TILE, width), lambda i: (i, 0))
    columns = pl.BlockSpec((width, HEAD), lambda i: (0, 1))
    return pl.pallas_call(
        project_kernel,
        grid=(token_count // TILE,),
        out_shape=jax.ShapeDtypeStruct(
            (parts, token_count // BLOCK, piece, 3 * HEAD), jnp.bfloat16
        ),
        in_specs=[rows, columns, columns, rows, pl.BlockSpec((HEAD, width), lambda i: (1, 0))],
        out_specs=pl.BlockSpec((parts, TILE // BLOCK, piece, 3 * HEAD), lambda i: (0, i, 0, 0)),
        name="project",
    )(tokens, shared_weight, value_weight, cotangent, output_weight)


def weight_terms(turned_rows, tokens_ref, cotangent_ref, scale, store):
    def step(part, carry):
        span = pl.ds(pl.multiple_of(part * TILE, TILE), TILE)
        terms = jnp.concatenate(
            [
                contract(turned_rows[HEAD:, :], tokens_ref[:, span], 1, 0),
                contract(turned_rows[:HEAD, :], cotangent_ref[:, span], 1, 0),
            ],
            axis=0,
        )
        store(part, (terms * scale).T.astype(jnp.bfloat16))
        return carry

    lax.fori_loop(0, tokens_ref.shape[1] // TILE, step, 0)


MESH = pl.DeviceIdType.MESH


def remote(source, target, send_sem, recv_sem, axis, peer):
    return pltpu.make_async_remote_copy(
        src_ref=source,
        dst_ref=target,
        send_sem=send_sem,
        recv_sem=recv_sem,
        device_id={axis: peer},
        device_id_type=MESH,
    )


def greet(barrier, axis, me, count):
    def step(number, carry):
        peer = lax.rem(me + number, count)
        pl.semaphore_signal(barrier, inc=1, device_id={axis: peer}, device_id_type=MESH)
        return carry

    lax.fori_loop(1, count, step, 0)


def start_kernel(
    seq_count,
    wide_count,
    leaving,
    marks,
    tokens_hbm,
    cotangent_hbm,
    shared_ref,
    value_ref,
    output_ref,
    middle,
    labels,
    local,
    before,
    after,
    shared_rows,
    value_rows,
    tokens_buf,
    cotangent_buf,
    load_sem,
    send_sem,
    recv_sem,
):
    me = lax.axis_index("seq")
    here = lax.axis_index("wide")
    load_tokens = pltpu.make_async_copy(tokens_hbm, tokens_buf, load_sem.at[0])
    load_cotangent = pltpu.make_async_copy(cotangent_hbm, cotangent_buf, load_sem.at[1])
    load_tokens.start()
    load_cotangent.start()
    barrier = pltpu.get_barrier_semaphore()
    greet(barrier, "seq", me, seq_count)
    greet(barrier, "wide", here, wide_count)
    pl.semaphore_wait(barrier, seq_count + wide_count - 2)

    def send(step, carry):
        peer = lax.rem(me + step, seq_count)
        remote(leaving.at[peer], middle.at[me], send_sem.at[0], recv_sem.at[0], "seq", peer).start()
        return carry

    lax.fori_loop(1, seq_count, send, 0)
    own = pltpu.make_async_copy(leaving.at[me], middle.at[me], load_sem.at[2])
    own.start()

    def send_marks(step, carry):
        peer = lax.rem(me + step, seq_count)
        remote(marks, labels.at[me], send_sem.at[1], recv_sem.at[1], "seq", peer).start()
        return carry

    lax.fori_loop(1, seq_count, send_marks, 0)
    labels[me] = marks[...]
    each = shared_rows.shape[1]

    def rows_of(owner):
        return pl.ds(pl.multiple_of(owner * each, each), each)

    for step in range(1, wide_count):
        peer = lax.rem(here + step, wide_count)
        rows = rows_of(peer)
        remote(
            shared_ref.at[rows], shared_rows.at[here], send_sem.at[2], recv_sem.at[2], "wide", peer
        ).start()
        remote(
            value_ref.at[rows], value_rows.at[here], send_sem.at[3], recv_sem.at[3], "wide", peer
        ).start()
    shared_rows[here] = shared_ref[rows_of(here), :]
    value_rows[here] = value_ref[rows_of(here), :]

    load_tokens.wait()
    load_cotangent.wait()
    tiles = local.shape[0] // TILE

    def make(tile):
        rows = pl.ds(tile * TILE, TILE)
        local[rows, :] = project_tile(
            tokens_buf[rows, :],
            cotangent_buf[rows, :],
            shared_ref.at[:, :HEAD],
            value_ref.at[:, :HEAD],
            output_ref.at[:HEAD, :],
        )

    make(tiles - 1)
    make(0)
    make(1)
    following = lax.rem(me + 1, seq_count)
    previous = lax.rem(me + seq_count - 1, seq_count)
    low = pl.ds((tiles - 1) * TILE, TILE)
    onward = remote(local.at[low], before, send_sem.at[4], recv_sem.at[4], "seq", following)
    backward = remote(local.at[pl.ds(0, TILE)], after, send_sem.at[5], recv_sem.at[5], "seq", previous)
    onward.start()
    backward.start()
    for tile in range(2, tiles - 1):
        make(tile)

    own.wait()
    peers = seq_count - 1
    sides = wide_count - 1
    many = middle.at[pl.ds(0, peers)]
    marked = labels.at[pl.ds(0, peers)]
    few = shared_rows.at[pl.ds(0, sides)]
    fewer = value_rows.at[pl.ds(0, sides)]
    waits = (
        remote(many, many, send_sem.at[0], recv_sem.at[0], "seq", following),
        remote(marked, marked, send_sem.at[1], recv_sem.at[1], "seq", following),
        remote(few, few, send_sem.at[2], recv_sem.at[2], "seq", following),
        remote(fewer, fewer, send_sem.at[3], recv_sem.at[3], "seq", following),
        onward,
        backward,
    )
    for copy in waits:
        copy.wait_recv()
    for copy in waits:
        copy.wait_send()


def start_step(leaving, marks, tokens, cotangent, shared_weight, value_weight, output_weight):
    seq_count = lax.axis_size("seq")
    wide_count = lax.axis_size("wide")
    count, width = tokens.shape
    own_width = shared_weight.shape[1]
    vmem = pl.BlockSpec(memory_space=pltpu.VMEM)
    anywhere = pl.BlockSpec(memory_space=pl.ANY)
    half = jnp.bfloat16
    halo = jax.ShapeDtypeStruct((WINDOW, 3 * HEAD), half)
    rows = jax.ShapeDtypeStruct((wide_count, width // wide_count, own_width), half)
    return pl.pallas_call(
        functools.partial(start_kernel, seq_count, wide_count),
        out_shape=(
            jax.ShapeDtypeStruct(leaving.shape, half),
            jax.ShapeDtypeStruct((seq_count,) + marks.shape, jnp.int32),
            jax.ShapeDtypeStruct((count, 3 * HEAD), half),
            halo,
            halo,
            rows,
            rows,
        ),
        in_specs=[anywhere, vmem, anywhere, anywhere, vmem, vmem, vmem],
        out_specs=(vmem,) * 7,
        scratch_shapes=[
            pltpu.VMEM((count, width), half),
            pltpu.VMEM((count, width), half),
            pltpu.SemaphoreType.DMA((3,)),
            pltpu.SemaphoreType.DMA((6,)),
            pltpu.SemaphoreType.DMA((6,)),
        ],
        compiler_params=pltpu.CompilerParams(collective_id=0, has_side_effects=True),
        name="start_step",
    )(leaving, marks, tokens, cotangent, shared_weight, value_weight, output_weight)


LAG = 3


def gather_and_send(me, seq_count, index_ref, source, staged, landing, each, send_sem, recv_sem):
    def pick(peer, store):
        for number in range(each):
            store(number, source[index_ref[peer * each + number]])

    def send(step):
        peer = lax.rem(me + step, seq_count)
        remote(staged.at[peer], landing.at[me], send_sem, recv_sem(step), "seq", peer).start()

    def step(number, carry):
        peer = lax.rem(me + number, seq_count)

        def store(slot, value):
            staged[peer, slot] = value

        pick(peer, store)

        @pl.when(number > LAG)
        def _():
            send(number - LAG)

        return carry

    lax.fori_loop(1, seq_count, step, 0)

    def keep(slot, value):
        landing[me, slot] = value

    pick(me, keep)
    for number in range(seq_count - LAG, seq_count):
        send(number)


def middle_kernel(
    seq_count,
    picked,
    middle,
    local,
    before,
    after,
    arrived,
    local_all,
    staged,
    ext,
    key_buf,
    query_sums,
    key_sums,
    value_sums,
    send_sem,
    recv_sem,
):
    me = lax.axis_index("seq")
    barrier = pltpu.get_barrier_semaphore()
    greet(barrier, "seq", me, seq_count)
    pl.semaphore_wait(barrier, seq_count - 1)
    gather_and_send(
        me,
        seq_count,
        picked,
        middle,
        staged,
        arrived,
        SLOTS,
        send_sem.at[0],
        lambda step: recv_sem.at[0],
    )
    band_body(
        me == 0,
        me == seq_count - 1,
        local,
        before,
        after,
        local_all,
        ext,
        key_buf,
        query_sums,
        key_sums,
        value_sums,
    )
    many = arrived.at[pl.ds(0, seq_count - 1)]
    done = remote(many, many, send_sem.at[0], recv_sem.at[0], "seq", lax.rem(me + 1, seq_count))
    done.wait_recv()
    done.wait_send()


def middle_step(picked, middle, local, before, after):
    seq_count = lax.axis_size("seq")
    piece = middle.shape[1]
    count = local.shape[0]
    rows = count + 2 * WINDOW
    vmem = pl.BlockSpec(memory_space=pltpu.VMEM)
    half = jnp.bfloat16
    shape = (seq_count, SLOTS, piece, 3 * HEAD)
    return pl.pallas_call(
        functools.partial(middle_kernel, seq_count),
        out_shape=(
            jax.ShapeDtypeStruct(shape, half),
            jax.ShapeDtypeStruct((count, 3 * HEAD), half),
        ),
        in_specs=[pl.BlockSpec(memory_space=pltpu.SMEM)] + [vmem] * 4,
        out_specs=(vmem, vmem),
        scratch_shapes=[
            pltpu.VMEM(shape, half),
            pltpu.VMEM((rows, 3 * HEAD), half),
            pltpu.VMEM((rows, HEAD), half),
            pltpu.VMEM((rows, HEAD), jnp.float32),
            pltpu.VMEM((rows, HEAD), jnp.float32),
            pltpu.VMEM((rows, HEAD), jnp.float32),
            pltpu.SemaphoreType.DMA((1,)),
            pltpu.SemaphoreType.DMA((1,)),
        ],
        compiler_params=pltpu.CompilerParams(collective_id=1, has_side_effects=True),
        name="middle_step",
    )(picked, middle, local, before, after)


GROUPS = 4


def final_kernel(
    seq_count,
    wide_count,
    scale,
    target,
    results,
    tokens_hbm,
    cotangent_hbm,
    local,
    shared_rows,
    value_rows,
    token_out,
    shared_out,
    value_out,
    output_out,
    back,
    staged,
    home,
    tokens_buf,
    cotangent_buf,
    rows_buf,
    turned_rows,
    local_left,
    local_right,
    local_far,
    from_left,
    from_right,
    from_far,
    total,
    local_pieces,
    local_arrived,
    pieces,
    arrived,
    load_sem,
    side_send,
    side_recv,
    home_recv,
    ring_send,
    ring_recv,
    bulk_send,
    bulk_recv,
):
    me = lax.axis_index("seq")
    here = lax.axis_index("wide")
    right = lax.rem(here + 1, wide_count)
    left = lax.rem(here + wide_count - 1, wide_count)
    far = lax.rem(here + 2, wide_count)
    following = lax.rem(me + 1, seq_count)
    slots = home.shape[1]
    count = rows_buf.shape[0]
    peers = seq_count - 1
    grads = pl.ds(HEAD, 2 * HEAD)

    load_tokens = pltpu.make_async_copy(tokens_hbm, tokens_buf, load_sem.at[0])
    load_cotangent = pltpu.make_async_copy(cotangent_hbm, cotangent_buf, load_sem.at[1])
    load_tokens.start()
    load_cotangent.start()
    barrier = pltpu.get_barrier_semaphore()
    for side in (left, right):
        pl.semaphore_signal(barrier, inc=1, device_id={"wide": side}, device_id_type=MESH)
    greet(barrier, "seq", me, seq_count)
    pl.semaphore_wait(barrier, peers + 2)

    def send_back(step, carry):
        peer = lax.rem(me + step, seq_count)
        remote(
            results.at[peer],
            back.at[pl.ds(me * SLOTS, SLOTS)],
            bulk_send.at[0],
            bulk_recv.at[0],
            "seq",
            peer,
        ).start()
        return carry

    lax.fori_loop(1, seq_count, send_back, 0)

    tops = pl.ds(0, count // 2)
    lows = pl.ds(count // 2, count // 2)

    def side(source, target_ref, number, peer):
        return remote(source, target_ref, side_send.at[number], side_recv.at[number], "wide", peer)

    right_top = side(local.at[tops, grads], local_left.at[tops], 0, right)
    right_low = side(local.at[lows, grads], local_left.at[lows], 1, right)
    left_top = side(local.at[tops, grads], local_right.at[tops], 2, left)
    left_low = side(local.at[lows, grads], local_right.at[lows], 3, left)
    onward_top = side(local_left.at[tops], local_far.at[tops], 4, right)
    onward_low = side(local_right.at[lows], local_far.at[lows], 5, left)
    right_top.start()
    left_low.start()
    right_low.start()
    left_top.start()

    back[pl.ds(me * SLOTS, SLOTS)] = results[me]
    turned_rows[...] = local[...].T
    load_tokens.wait()
    load_cotangent.wait()
    rows_each = pieces.shape[1]
    per_part = TILE // rows_each

    def storing(buffer):
        def store(part, terms):
            buffer[pl.ds(part * per_part, per_part)] = terms.reshape(per_part, rows_each, 3 * HEAD)

        return store

    weight_terms(turned_rows, tokens_buf, cotangent_buf, scale, storing(local_pieces))
    right_top.wait_recv()
    onward_top.start()
    left_low.wait_recv()
    onward_low.start()

    all_back = back.at[pl.ds(0, peers * SLOTS)]
    back_done = remote(all_back, all_back, bulk_send.at[0], bulk_recv.at[0], "seq", following)
    back_done.wait_recv()

    group_size = seq_count // GROUPS

    def group_of(step):
        return step // group_size

    gather_and_send(
        me,
        seq_count,
        target,
        back,
        staged,
        home,
        slots,
        bulk_send.at[1],
        lambda step: home_recv.at[group_of(step)],
    )

    def piece_copy(buffer, landing, number, peer):
        return remote(
            buffer.at[peer], landing.at[me], bulk_send.at[number], bulk_recv.at[number], "seq", peer
        )

    def send_local(step, carry):
        piece_copy(local_pieces, local_arrived, 2, lax.rem(me + step, seq_count)).start()
        return carry

    lax.fori_loop(1, seq_count, send_local, 0)

    def add_terms(source, owner, head, first, last):
        columns = pl.ds(head * HEAD, HEAD)
        weights = jnp.concatenate(
            [shared_rows[owner, :, columns], value_rows[owner, :, columns]], axis=1
        )

        def step(slot, carry):
            span = pl.ds(pl.multiple_of(slot * BLOCK, BLOCK), BLOCK)
            value = contract(source(slot, span), weights, 1, 1)
            if not first:
                value = value + total[span, :]
            if last:
                token_out[span, :] = value.astype(jnp.bfloat16)
            else:
                total[span, :] = value
            return carry

        lax.fori_loop(0, slots, step, 0, unroll=2)

    add_terms(lambda slot, span: local[span, HEAD:], here, 0, True, False)
    right_low.wait_recv()
    add_terms(lambda slot, span: local_left[span, :], left, 0, False, False)
    left_top.wait_recv()
    add_terms(lambda slot, span: local_right[span, :], right, 0, False, False)
    onward_top.wait_recv()
    onward_low.wait_recv()
    add_terms(lambda slot, span: local_far[span, :], far, 0, False, False)

    def ring(number, group, source, target_ref, peer):
        spot = number * GROUPS + group
        return remote(source, target_ref, ring_send.at[spot], ring_recv.at[spot], "wide", peer)

    def ring_all(number, group, buffer, target_buffer, peer):
        def step(place, carry):
            chunk = lax.rem(me + seq_count - group * group_size - place, seq_count)
            if buffer.shape[3] == 2 * HEAD:
                source = buffer.at[chunk]
            else:
                source = buffer.at[chunk, :, :, grads]
            ring(number, group, source, target_buffer.at[chunk], peer).start()
            return carry

        lax.fori_loop(0, group_size, step, 0)

    def ring_done(number, group, buffer):
        whole = buffer.at[pl.ds(0, group_size)]
        return ring(number, group, whole, whole, right)

    def home_done(group):
        size = group_size - 1 if group == 0 else group_size
        whole = home.at[pl.ds(0, size)]
        return remote(whole, whole, bulk_send.at[1], home_recv.at[group], "seq", following)

    def forward(group):
        if group % 2 == 0:
            ring_done(0, group, from_left).wait_recv()
            ring_all(2, group, from_left, from_far, right)
        else:
            ring_done(1, group, from_right).wait_recv()
            ring_all(2, group, from_right, from_far, left)

    for group in range(GROUPS):
        home_done(group).wait_recv()
        ring_all(0, group, home, from_left, right)
        ring_all(1, group, home, from_right, left)

    def merge(slot, carry):
        span = pl.ds(pl.multiple_of(slot * BLOCK, BLOCK), BLOCK)
        rows = home[:, slot].reshape(BLOCK, 3 * HEAD)
        rows_buf[span, :] = rows
        turned_rows[:, span] = rows.T
        return carry

    lax.fori_loop(0, slots, merge, 0, unroll=2)
    forward(0)
    forward(1)
    weight_terms(turned_rows, tokens_buf, cotangent_buf, scale, storing(pieces))

    def send_piece(step, carry):
        piece_copy(pieces, arrived, 3, lax.rem(me + step, seq_count)).start()
        return carry

    lax.fori_loop(1, seq_count, send_piece, 0)
    forward(2)
    forward(3)

    def merged(buffer):
        return lambda slot, span: buffer[:, slot].reshape(BLOCK, 2 * HEAD)

    add_terms(lambda slot, span: rows_buf[span, HEAD:], here, 1, False, False)
    ring_done(0, 1, from_left).wait_recv()
    ring_done(0, 3, from_left).wait_recv()
    add_terms(merged(from_left), left, 1, False, False)
    ring_done(1, 0, from_right).wait_recv()
    ring_done(1, 2, from_right).wait_recv()
    add_terms(merged(from_right), right, 1, False, False)

    def sums_of(number, buffer, landing):
        whole = landing.at[pl.ds(0, peers)]
        done = remote(whole, whole, bulk_send.at[number], bulk_recv.at[number], "seq", following)
        done.wait_recv()

        def step(place, sums):
            return sums + landing[lax.rem(me + place, seq_count)].astype(jnp.float32)

        return lax.fori_loop(1, seq_count, step, buffer[me].astype(jnp.float32)), done

    local_sums, local_done = sums_of(2, local_pieces, local_arrived)
    for group in range(GROUPS):
        ring_done(2, group, from_far).wait_recv()
    add_terms(merged(from_far), far, 1, False, True)
    routed_sums, routed_done = sums_of(3, pieces, arrived)

    def paired(number):
        columns = slice(number * HEAD, (number + 1) * HEAD)
        return jnp.concatenate([local_sums[:, columns], routed_sums[:, columns]], axis=1)

    shared_out[...] = paired(0)
    value_out[...] = paired(1)
    output_out[...] = paired(2)

    for copy in (right_top, right_low, left_top, left_low, onward_top, onward_low):
        copy.wait_send()
    back_done.wait_send()
    whole_home = home.at[pl.ds(0, peers)]
    remote(whole_home, whole_home, bulk_send.at[1], bulk_recv.at[1], "seq", following).wait_send()
    local_done.wait_send()
    routed_done.wait_send()
    for number in range(3):
        for group in range(GROUPS):
            ring_done(number, group, from_far).wait_send()


def final_step(target, results, tokens, cotangent, local_all, shared_rows, value_rows, scale):
    count, width = tokens.shape
    seq_count = lax.axis_size("seq")
    wide_count = lax.axis_size("wide")
    each = width // seq_count
    out_width = width // wide_count
    slots = count // BLOCK
    piece = results.shape[2]
    half = jnp.bfloat16
    vmem = pl.BlockSpec(memory_space=pltpu.VMEM)
    anywhere = pl.BlockSpec(memory_space=pl.ANY)
    small = jax.ShapeDtypeStruct((each, 2 * HEAD), jnp.float32)
    full = pltpu.VMEM((seq_count, slots, piece, 3 * HEAD), half)
    chunk = pltpu.VMEM((seq_count, slots, piece, 2 * HEAD), half)
    flat = pltpu.VMEM((count, 2 * HEAD), half)
    terms = pltpu.VMEM((seq_count, each, 3 * HEAD), half)
    return pl.pallas_call(
        functools.partial(final_kernel, seq_count, wide_count, scale),
        out_shape=(jax.ShapeDtypeStruct((count, out_width), half), small, small, small),
        in_specs=[pl.BlockSpec(memory_space=pltpu.SMEM), vmem, anywhere, anywhere, vmem, vmem, vmem],
        out_specs=(vmem,) * 4,
        scratch_shapes=[
            pltpu.VMEM((seq_count * SLOTS, piece, 3 * HEAD), half),
            full,
            full,
            pltpu.VMEM((count, width), half),
            pltpu.VMEM((count, width), half),
            pltpu.VMEM((count, 3 * HEAD), half),
            pltpu.VMEM((3 * HEAD, count), half),
            flat,
            flat,
            flat,
            chunk,
            chunk,
            chunk,
            pltpu.VMEM((count, out_width), jnp.float32),
            terms,
            terms,
            terms,
            terms,
            pltpu.SemaphoreType.DMA((2,)),
            pltpu.SemaphoreType.DMA((6,)),
            pltpu.SemaphoreType.DMA((6,)),
            pltpu.SemaphoreType.DMA((GROUPS,)),
            pltpu.SemaphoreType.DMA((3 * GROUPS,)),
            pltpu.SemaphoreType.DMA((3 * GROUPS,)),
            pltpu.SemaphoreType.DMA((4,)),
            pltpu.SemaphoreType.DMA((4,)),
        ],
        compiler_params=pltpu.CompilerParams(collective_id=2, has_side_effects=True),
        name="final_step",
    )(target, results, tokens, cotangent, local_all, shared_rows, value_rows)


def on_device(tokens, shared_weight, value_weight, output_weight, cotangent, block_clusters):
    seq_count = lax.axis_size("seq")
    position = lax.axis_index("seq")
    token_count = tokens.shape[0]
    block_count = token_count // BLOCK
    piece = BLOCK // seq_count
    grad_scale = 1.0 / math.sqrt(seq_count * token_count)

    leaving = project(tokens, shared_weight, value_weight, cotangent, output_weight, seq_count)
    marks = jnp.pad(block_clusters, ((0, 7), (0, HEAD - block_count)))
    middle, labels, local, before, after, shared_rows, value_rows = start_step(
        leaving, marks, tokens, cotangent, shared_weight, value_weight, output_weight
    )
    labels = labels[:, 0, :block_count].reshape(seq_count * block_count)
    target, picked, first = route(labels, seq_count, block_count)
    middle = middle.reshape(seq_count * block_count, piece, 3 * HEAD)
    arrived, local_all = middle_step(picked, middle, local, before, after)
    own_first = lax.dynamic_slice_in_dim(first, position * SLOTS, SLOTS, 0)
    results = cluster_attention(own_first, arrived)
    token_grads, shared_grads, value_grads, output_grads = final_step(
        target, results, tokens, cotangent, local_all, shared_rows, value_rows, grad_scale
    )
    return token_grads, shared_grads, value_grads, output_grads.T


def solution(mesh):
    placed = (
        P("seq", None),
        P(None, "wide"),
        P(None, "wide"),
        P("wide", None),
        P("seq", None),
        P("wide", "seq"),
    )
    return jax.shard_map(
        on_device,
        mesh=mesh,
        in_specs=placed,
        out_specs=(P("seq", "wide"), P("seq", "wide"), P("seq", "wide"), P("wide", "seq")),
        check_vma=False,
    )
```
